256 devices in a mesh: gx: 8 (over x, core), gy: 4 (over y), gz: 8 (over z).
Axes of the slice: x: 4, y: 4, z: 8, core: 2. Of those that a mesh axis runs over, the one named last changes fastest.
Arguments:
- right_side: float32 [3, 64, 32, 64, 128], P(None, 'gx', 'gy', 'gz'), may hold values from -24 to 24
- stiffness: float32 [3, 64, 32, 64], P(None, 'gx', 'gy', 'gz'), may hold values from 0.25 to 4
- local_factor: bfloat16 [8, 4, 8, 2048, 2048], P('gx', 'gy', 'gz'), as said below
- basis: bfloat16 [8, 4, 8, 64, 1536], P('gx', 'gy', 'gz'), may hold values from -0.3125 to 0.3125
- coarse_map: int32 [8, 4, 8, 64], P('gx', 'gy', 'gz'), may hold values from 0 to 63, each once within a row
- margin_index: int32 [8, 4, 8, 512], P('gx', 'gy', 'gz'), may hold values from 0 to 1151, as said below
- coarse_inverse: bfloat16 [16384, 16384], P(('gx', 'gy', 'gz')), as said below
Outputs:
- solution: float32 [3, 64, 32, 64, 128], P(None, 'gx', 'gy', 'gz')
- residual_ratio: float32 [128], replicated
The draws below stay inside these ranges and needn't reach their ends.
Inputs may be any that keep to these rules, and one draw needn't show every extreme that they name: `local_factor`: each subdomain's factor is zero above its diagonal. coarse_inverse is symmetric. `margin_index`: within each subdomain the 512 entries are distinct and increasing. `coarse_map`: each subdomain's entries are a permutation of 0 to 63.
All inputs are finite; a program needn't handle non-finite values.
Results may differ from the reference program's by a relative error of at most 0.0055.
Values may be sent and summed in bfloat16 or wider, within the bound.
No kernel may reach another device: no remote copies, remote signals or barrier semaphores. Data moves between devices by JAX's collectives and lax.ppermute only.
A program may use at most 64 MiB of HBM per device.

```python
import math
import jax
import jax.numpy as jnp
from jax import lax

CX = 8
CY = 8
CZ = 8
R = 128
LOC = 2048
CB = 64
OWN = 1536
OVL = 512
HALO_DOFS = 1152
COARSE = 16384
NX = 64
NY = 32
NZ = 64
N_GX = 8
N_GY = 4
N_GZ = 8


def draw_local_factor(key, part):
    sub_count = NX // CX * (NY // CY) * (NZ // CZ)
    sub_keys = jax.random.split(key, sub_count)
    row_ids = lax.broadcasted_iota(jnp.int32, (LOC, LOC), 0)
    col_ids = lax.broadcasted_iota(jnp.int32, (LOC, LOC), 1)

    def one_factor(sub_key):
        key_low, key_high = jax.random.split(sub_key)
        spread = jax.random.normal(key_low, (LOC, LOC), jnp.float32)
        diagonal = jax.random.uniform(key_high, (LOC,), jnp.float32, 0.75, 1.25)
        below = jnp.where(col_ids < row_ids, spread * (0.6 / math.sqrt(LOC)), 0.0)
        return (below + jnp.where(col_ids == row_ids, diagonal[:, None], 0.0)).astype(jnp.bfloat16)
    return lax.map(one_factor, sub_keys).reshape(NX // CX, NY // CY, NZ // CZ, LOC, LOC)


def draw_margin_index(key, part):
    sub_count = NX // CX * (NY // CY) * (NZ // CZ)
    sub_keys = jax.random.split(key, sub_count)

    def one_choice(sub_key):
        shuffled = jax.random.permutation(sub_key, HALO_DOFS - 2) + 1
        chosen = jnp.sort(shuffled[:OVL - 2]).astype(jnp.int32)
        return jnp.concatenate([jnp.zeros((1,), jnp.int32), chosen, jnp.full((1,), HALO_DOFS - 1, jnp.int32)])
    return jax.vmap(one_choice)(sub_keys).reshape(NX // CX, NY // CY, NZ // CZ, OVL)


def draw_coarse_inverse(key, part):
    key_low, key_high = jax.random.split(key)
    raw_draw = jax.random.normal(key_low, (COARSE, COARSE), jnp.float32)
    row_ids = lax.broadcasted_iota(jnp.int32, (COARSE, COARSE), 0)
    col_ids = lax.broadcasted_iota(jnp.int32, (COARSE, COARSE), 1)
    symmetric = (raw_draw + raw_draw.T) * (0.4 / math.sqrt(2.0 * COARSE))
    diagonal = jax.random.uniform(key_high, (COARSE,), jnp.float32, 0.8, 1.2)
    return (symmetric + jnp.where(row_ids == col_ids, diagonal[:, None], 0.0)).astype(jnp.bfloat16)


def block_levels(key, extent, shards, low, top_value):
    def one(axis_at, parts):
        draws = jax.random.uniform(jax.random.fold_in(jax.random.fold_in(key, 6), axis_at), (parts,), jnp.float32, low / len(shards), top_value / len(shards))
        return jnp.repeat(jnp.exp(draws), extent[axis_at] // parts).reshape((-1,) + (1,) * (len(extent) - axis_at - 1))

    gain = one(*shards[0])
    for cut in shards[1:]:
        gain = gain * one(*cut)
    return gain


def normal_values(own_key, dims, scale, bound, cuts=(), kind=jnp.bfloat16):
    level = block_levels(own_key, dims, cuts, -0.22, 0.18) if cuts else 1.0
    entries = jax.random.normal(own_key, dims, jnp.float32) * scale * level
    return jnp.minimum(jnp.maximum(entries, -bound), bound).astype(kind)


def setup_inputs(seed: int = 0) -> dict:
    arg_keys = jax.random.split(jax.random.key(seed), 8)
    return {
        "right_side": normal_values(arg_keys[0], (3, NX, NY, NZ, R), 4.0, 24.0, ((1, 8), (2, 4), (3, 8)), jnp.float32),
        "stiffness": jnp.clip(jnp.exp(math.log(4.0) - 2.7725887 * jax.random.uniform(arg_keys[1], (3, NX, NY, NZ), jnp.float32) ** block_levels(arg_keys[1], (3, NX, NY, NZ), ((1, 8), (2, 4), (3, 8)), -0.2, 0.2)), 0.25, 4.0),
        "local_factor": draw_local_factor(jax.random.fold_in(arg_keys[7], 71), 0),
        "basis": normal_values(arg_keys[3], (N_GX, N_GY, N_GZ, CB, OWN), (OWN // 4) ** -0.5, 0.3125, ((0, 8), (1, 4), (2, 8))),
        "coarse_map": jax.vmap(lambda own: jax.random.permutation(own, CB))(jax.random.split(arg_keys[4], N_GX * N_GY * N_GZ)).reshape((N_GX, N_GY, N_GZ, CB)).astype(jnp.int32),
        "margin_index": draw_margin_index(jax.random.fold_in(arg_keys[7], 71), 0),
        "coarse_inverse": draw_coarse_inverse(jax.random.fold_in(arg_keys[7], 71), 0),
    }


EPSILON = 1e-06

def inner(left, right):
    return lax.optimization_barrier(jnp.sum(left * right, axis=(0, 1, 2, 3)))

def face_rows(padded):
    rhs_count = padded.shape[-1]
    slabs = [padded[:, 0, 1:-1, 1:-1], padded[:, -1, 1:-1, 1:-1], padded[:, 1:-1, 0, 1:-1], padded[:, 1:-1, -1, 1:-1], padded[:, 1:-1, 1:-1, 0], padded[:, 1:-1, 1:-1, -1]]
    joined = jnp.concatenate([slab.reshape(slab.shape[0], -1, rhs_count) for slab in slabs], axis=1)
    return joined.reshape(-1, rhs_count)

def operate(field, stiffness):
    padded = jnp.pad(field, ((0, 0), (1, 1), (1, 1), (1, 1), (0, 0)))
    beside = padded[:, 2:, 1:-1, 1:-1] + padded[:, :-2, 1:-1, 1:-1]
    beside = beside + padded[:, 1:-1, 2:, 1:-1] + padded[:, 1:-1, :-2, 1:-1]
    beside = beside + padded[:, 1:-1, 1:-1, 2:] + padded[:, 1:-1, 1:-1, :-2]
    return (6.0 + stiffness[..., None]) * field - beside

def reference(right_side, stiffness, local_factor, basis, coarse_map, margin_index, coarse_inverse):
    x_parts = NX // CX
    y_parts = NY // CY
    z_parts = NZ // CZ
    devices = x_parts * y_parts * z_parts
    factors = local_factor.reshape(devices, LOC, LOC)
    bases = basis.reshape(devices, CB, OWN)
    coarse_maps = coarse_map.reshape(devices, CB).astype(jnp.int32)
    margin_picks = margin_index.reshape(devices, OVL).astype(jnp.int32)
    offsets = jnp.arange(devices, dtype=jnp.int32) * CB
    targets = (offsets[:, None] + coarse_maps).astype(jnp.int32)
    device_ids = jnp.arange(devices, dtype=jnp.int32)

    def to_blocks(field):
        shaped = field.reshape(3, x_parts, CX, y_parts, CY, z_parts, CZ, R)
        return shaped.transpose(1, 3, 5, 0, 2, 4, 6, 7).reshape(devices, OWN, R)

    def from_blocks(blocks):
        shaped = blocks.reshape(x_parts, y_parts, z_parts, 3, CX, CY, CZ, R)
        return shaped.transpose(3, 0, 4, 1, 5, 2, 6, 7).reshape(3, NX, NY, NZ, R)

    def precondition(field):
        rounded = field.astype(jnp.bfloat16)
        padded = jnp.pad(rounded, ((0, 0), (1, 1), (1, 1), (1, 1), (0, 0)))
        own_all = to_blocks(rounded)

        def local_solve(device_index):
            x_index = device_index // (y_parts * z_parts)
            y_index = device_index // z_parts % y_parts
            z_index = device_index % z_parts
            anchor = jnp.int32(0)
            block = lax.dynamic_slice(padded, (anchor, (x_index * CX).astype(jnp.int32), (y_index * CY).astype(jnp.int32), (z_index * CZ).astype(jnp.int32), anchor), (3, CX + 2, CY + 2, CZ + 2, R))
            own_rows = own_all[device_index]
            extended = jnp.concatenate([own_rows, jnp.take(face_rows(block), margin_picks[device_index], axis=0)], axis=0)
            factor = factors[device_index]
            front_values = jnp.dot(factor, extended, preferred_element_type=jnp.float32).astype(jnp.bfloat16)
            back_sweep = jnp.dot(factor.T, front_values, preferred_element_type=jnp.float32)[:OWN]
            restricted = jnp.dot(bases[device_index], own_rows, preferred_element_type=jnp.float32)
            return (back_sweep, restricted)
        local_parts, restricted = lax.map(local_solve, device_ids)
        coarse_residual = jnp.zeros((COARSE, R), jnp.float32).at[targets.reshape(-1)].set(restricted.reshape(-1, R)).astype(jnp.bfloat16)
        coarse_solution = jnp.dot(coarse_inverse, coarse_residual, preferred_element_type=jnp.float32).astype(jnp.bfloat16)
        picked = coarse_solution[targets]

        def prolong(device_index):
            return jnp.dot(bases[device_index].T, picked[device_index], preferred_element_type=jnp.float32)
        coarse_parts = lax.map(prolong, device_ids)
        return from_blocks(local_parts + coarse_parts)
    start_norm = jnp.sqrt(inner(right_side, right_side) + EPSILON)
    basis_one = right_side / start_norm
    search_one = precondition(basis_one)
    image_one = operate(search_one, stiffness)
    along_one = inner(image_one, basis_one)
    rest_one = image_one - along_one * basis_one
    norm_two = jnp.sqrt(inner(rest_one, rest_one) + EPSILON)
    basis_two = rest_one / norm_two
    search_two = precondition(basis_two)
    image_two = operate(search_two, stiffness)
    cross_two = inner(image_two, basis_one)
    along_two = inner(image_two, basis_two)
    rest_two = image_two - cross_two * basis_one - along_two * basis_two
    norm_three = jnp.sqrt(inner(rest_two, rest_two) + EPSILON)
    radius_one = jnp.sqrt(along_one * along_one + norm_two * norm_two)
    cosine_one = along_one / radius_one
    sine_one = norm_two / radius_one
    turned_one = cosine_one * cross_two + sine_one * along_two
    turned_two = cosine_one * along_two - sine_one * cross_two
    radius_two = jnp.sqrt(turned_two * turned_two + norm_three * norm_three)
    cosine_two = turned_two / radius_two
    sine_two = norm_three / radius_two
    coef_two = -cosine_two * sine_one * start_norm / radius_two
    coef_one = (cosine_one * start_norm - turned_one * coef_two) / radius_one
    solution = coef_one * search_one + coef_two * search_two
    return (solution, sine_one * sine_two)
```

```python
import jax
import jax.numpy as jnp
from jax import lax
from jax.sharding import Mesh
from jax.sharding import PartitionSpec as P

GX_GY_GZ = ("gx_0", "gx_1", "gy", "gz")
GX = ("gx_0", "gx_1")


EPSILON = 1e-06
SCALE = 2.0**-14


def extended_2(value, sides, width):
    edges = {}
    for axis, dim in sides:
        peers, length = (lax.axis_size(axis), value.shape[dim])
        up = [(i, (i + 1) % peers) for i in range(peers - 1)]
        last = lax.slice_in_dim(value, length - width, length, axis=dim)
        leading = lax.slice_in_dim(value, 0, width, axis=dim)
        edges[dim] = (
            lax.ppermute(last, axis, up),
            lax.ppermute(leading, axis, [(b, a) for a, b in up]),
        )
    done = []
    for _, dim in sides:
        low, high = edges[dim]
        around = [(width, width) if d in done else (0, 0) for d in range(value.ndim)]
        value = jnp.concatenate([jnp.pad(low, around), value, jnp.pad(high, around)], axis=dim)
        done.append(dim)
    return value


def inner(left, right):
    return jnp.sum(left * right, axis=(0, 1, 2, 3))


def face_rows(padded):
    rhs_count = padded.shape[-1]
    slabs = [
        padded[:, 0, 1:-1, 1:-1],
        padded[:, -1, 1:-1, 1:-1],
        padded[:, 1:-1, 0, 1:-1],
        padded[:, 1:-1, -1, 1:-1],
        padded[:, 1:-1, 1:-1, 0],
        padded[:, 1:-1, 1:-1, -1],
    ]
    joined = jnp.concatenate([slab.reshape(slab.shape[0], -1, rhs_count) for slab in slabs], axis=1)
    return joined.reshape(-1, rhs_count)


def weights(gram):
    raw_raw, one_raw, one_one, two_raw, two_one, two_two = (gram[i] for i in range(6))
    start_square = raw_raw / (SCALE * SCALE) + EPSILON
    start_norm = jnp.sqrt(start_square)
    size = start_norm * SCALE
    square = size * size
    kept = raw_raw / square
    along_one = one_raw / square
    rest_one = one_one / square - along_one * along_one * (2.0 - kept)
    rest_one = jnp.maximum(rest_one, 0.0) + EPSILON
    norm_two = jnp.sqrt(rest_one)
    kept_two = (rest_one - EPSILON) / rest_one
    shared = along_one * (1.0 - kept) / norm_two
    cross_two = (two_raw - along_one * one_raw) / (square * norm_two)
    along_two = (
        (two_one - along_one * two_raw) - along_one * (one_one - along_one * one_raw)
    ) / (square * rest_one)
    image_square = (two_two - along_one * (2.0 * two_one - along_one * one_one)) / (
        square * rest_one
    )
    rest_two = (
        image_square
        - cross_two * cross_two * (2.0 - kept)
        - along_two * along_two * (2.0 - kept_two)
        + 2.0 * cross_two * along_two * shared
    )
    norm_three = jnp.sqrt(jnp.maximum(rest_two, 0.0) + EPSILON)
    radius_one = jnp.sqrt(along_one * along_one + norm_two * norm_two)
    cosine_one = along_one / radius_one
    sine_one = norm_two / radius_one
    turned_one = cosine_one * cross_two + sine_one * along_two
    turned_two = cosine_one * along_two - sine_one * cross_two
    radius_two = jnp.sqrt(turned_two * turned_two + norm_three * norm_three)
    cosine_two = turned_two / radius_two
    sine_two = norm_three / radius_two
    coef_two = -cosine_two * sine_one * start_norm / radius_two
    coef_one = (cosine_one * start_norm - turned_one * coef_two) / radius_one
    weight_two = coef_two / (size * norm_two)
    weight_one = coef_one / size - along_one * weight_two
    return (weight_one, weight_two, sine_one * sine_two)


def local(right_side, stiffness, local_factor, basis, coarse_map, margin_index, coarse_inverse):
    factor = local_factor.reshape(local_factor.shape[-2:])
    coarse_basis = basis.reshape(basis.shape[-2:])
    basis_count = coarse_basis.shape[0]
    coarse_ids = coarse_map.reshape(-1)
    margin_rows = margin_index.reshape(-1)
    placement_table = (
        coarse_ids[None, :] == lax.broadcasted_iota(jnp.int32, (basis_count, basis_count), 0)
    ).astype(jnp.float32)
    contract_first = (((0,), (0,)), ((), ()))

    def precondition(field):
        rounded = field.astype(jnp.bfloat16)
        padded = extended_2(rounded, ((GX, 1), ("gy", 2), ("gz", 3)), 1)
        own_rows = rounded.reshape(-1, rounded.shape[-1])
        extended = jnp.concatenate(
            [own_rows, jnp.take(face_rows(padded), margin_rows, axis=0)], axis=0
        )
        front_values = jnp.dot(factor, extended, preferred_element_type=jnp.float32).astype(
            jnp.bfloat16
        )
        back_sweep = lax.dot_general(
            factor, front_values, contract_first, preferred_element_type=jnp.float32
        )
        local_part = back_sweep[: own_rows.shape[0]]
        restricted = jnp.dot(coarse_basis, own_rows, preferred_element_type=jnp.float32)
        placed = jnp.dot(placement_table, restricted, precision=lax.Precision.HIGHEST).astype(
            jnp.bfloat16
        )
        solved = jnp.dot(
            coarse_inverse,
            lax.all_gather(placed, GX_GY_GZ, tiled=True),
            preferred_element_type=jnp.float32,
        )
        solved = solved.astype(jnp.bfloat16)
        own_coarse = lax.dot_general(
            placement_table,
            solved.astype(jnp.float32),
            contract_first,
            precision=lax.Precision.HIGHEST,
        ).astype(jnp.bfloat16)
        coarse_part = lax.dot_general(
            coarse_basis, own_coarse, contract_first, preferred_element_type=jnp.float32
        )
        return (local_part + coarse_part).reshape(field.shape)

    def operate(field):
        padded = extended_2(field.astype(jnp.bfloat16), ((GX, 1), ("gy", 2), ("gz", 3)), 1).astype(
            field.dtype
        )
        beside = padded[:, 2:, 1:-1, 1:-1] + padded[:, :-2, 1:-1, 1:-1]
        beside = beside + padded[:, 1:-1, 2:, 1:-1] + padded[:, 1:-1, :-2, 1:-1]
        beside = beside + padded[:, 1:-1, 1:-1, 2:] + padded[:, 1:-1, 1:-1, :-2]
        return (6.0 + stiffness[..., None]) * field - beside

    raw = right_side * SCALE
    search_one = precondition(raw)
    image_one = operate(search_one)
    search_two = precondition(image_one)
    image_two = operate(search_two)
    gram = lax.psum(
        jnp.stack(
            [
                inner(raw, raw),
                inner(image_one, raw),
                inner(image_one, image_one),
                inner(image_two, raw),
                inner(image_two, image_one),
                inner(image_two, image_two),
            ]
        ),
        GX_GY_GZ,
    )
    weight_one, weight_two, ratio = weights(gram)
    return (weight_one * search_one + weight_two * search_two, ratio)


def solution(mesh):
    finer = Mesh(
        mesh.devices.reshape(4, 2, mesh.shape["gy"], mesh.shape["gz"]), ("gx_0", "gx_1", "gy", "gz")
    )
    placed = (
        P(None, GX, "gy", "gz", None),
        P(None, GX, "gy", "gz"),
        P(GX, "gy", "gz", None, None),
        P(GX, "gy", "gz", None, None),
        P(GX, "gy", "gz", None),
        P(GX, "gy", "gz", None),
        P(GX_GY_GZ, None),
    )
    return jax.shard_map(
        local,
        mesh=finer,
        in_specs=placed,
        out_specs=(P(None, GX, "gy", "gz", None), P()),
        check_vma=False,
    )
```

```python
import jax
import jax.numpy as jnp
from jax import lax
from jax.experimental import pallas as pl
from jax.experimental.pallas import tpu as pltpu
from jax.sharding import Mesh
from jax.sharding import PartitionSpec as P


X, C, Y, Z = "gx_0", "gx_1", "gy", "gz"
GX = (X, C)
GX_GY_GZ = (X, C, Y, Z)

EPSILON = 1e-06
SCALE = 2.0**-14
TILE = 256


def shift(value, axis, step):
    count = lax.axis_size(axis)
    return lax.ppermute(value, axis, [(i, (i + step) % count) for i in range(count)])


def halo(blocks):
    lanes = blocks.shape[-1]
    faces = []
    for axis, dim in ((GX, 1), (Y, 2), (Z, 3)):
        peers, length = (lax.axis_size(axis), blocks.shape[dim])
        up = [(i, i + 1) for i in range(peers - 1)]
        last = lax.slice_in_dim(blocks, length - 1, length, axis=dim).reshape(-1, lanes)
        first = lax.slice_in_dim(blocks, 0, 1, axis=dim).reshape(-1, lanes)
        faces.append(lax.ppermute(last, axis, up))
        faces.append(lax.ppermute(first, axis, [(b, a) for a, b in up]))
    return faces


def inner(left, right):
    return jnp.sum(left * right, axis=(0, 1, 2, 3))


def weights(gram):
    raw_raw, one_raw, one_one, two_raw, two_one, two_two = (gram[i] for i in range(6))
    start_square = raw_raw / (SCALE * SCALE) + EPSILON
    start_norm = jnp.sqrt(start_square)
    size = start_norm * SCALE
    square = size * size
    kept = raw_raw / square
    along_one = one_raw / square
    rest_one = one_one / square - along_one * along_one * (2.0 - kept)
    rest_one = jnp.maximum(rest_one, 0.0) + EPSILON
    norm_two = jnp.sqrt(rest_one)
    kept_two = (rest_one - EPSILON) / rest_one
    shared = along_one * (1.0 - kept) / norm_two
    cross_two = (two_raw - along_one * one_raw) / (square * norm_two)
    along_two = (
        (two_one - along_one * two_raw) - along_one * (one_one - along_one * one_raw)
    ) / (square * rest_one)
    image_square = (two_two - along_one * (2.0 * two_one - along_one * one_one)) / (
        square * rest_one
    )
    rest_two = (
        image_square
        - cross_two * cross_two * (2.0 - kept)
        - along_two * along_two * (2.0 - kept_two)
        + 2.0 * cross_two * along_two * shared
    )
    norm_three = jnp.sqrt(jnp.maximum(rest_two, 0.0) + EPSILON)
    radius_one = jnp.sqrt(along_one * along_one + norm_two * norm_two)
    cosine_one = along_one / radius_one
    sine_one = norm_two / radius_one
    turned_one = cosine_one * cross_two + sine_one * along_two
    turned_two = cosine_one * along_two - sine_one * cross_two
    radius_two = jnp.sqrt(turned_two * turned_two + norm_three * norm_three)
    cosine_two = turned_two / radius_two
    sine_two = norm_three / radius_two
    coef_two = -cosine_two * sine_one * start_norm / radius_two
    coef_one = (cosine_one * start_norm - turned_one * coef_two) / radius_one
    weight_two = coef_two / (size * norm_two)
    weight_one = coef_one / size - along_one * weight_two
    return (weight_one, weight_two, sine_one * sine_two)


def local_kernel(order, own, *rest):
    faces, (factor, out, held, stacked, front, ring, done) = rest[:6], rest[6:]
    size = stacked.shape[0]
    own_count = own.shape[0]
    tiles = size // TILE

    def copy(i):
        rows, width = pl.ds(i * TILE, TILE), (i + 1) * TILE
        return pltpu.make_async_copy(
            factor.at[rows, pl.ds(0, width)], held.at[rows, pl.ds(0, width)], done.at[i]
        )

    for i in range(tiles):
        copy(i).start()
    stacked[:own_count] = own[...]
    per_part = faces[0].shape[0] // 3
    for part in range(3):
        for k, face in enumerate(faces):
            ring[pl.ds((part * 6 + k) * per_part, per_part)] = face[
                pl.ds(part * per_part, per_part)
            ]
    picks = order.shape[0]
    table = lax.broadcasted_iota(jnp.int32, (picks, ring.shape[0]), 1) == order[...]
    stacked[own_count:] = jnp.dot(
        table.astype(jnp.float32).astype(jnp.bfloat16),
        ring[...],
        preferred_element_type=jnp.float32,
    ).astype(jnp.bfloat16)
    for i in range(tiles):
        copy(i).wait()
        width = (i + 1) * TILE
        front[pl.ds(i * TILE, TILE)] = jnp.dot(
            held[pl.ds(i * TILE, TILE), :width],
            stacked[:width],
            preferred_element_type=jnp.float32,
        ).astype(jnp.bfloat16)
    for j in range(own_count // TILE):
        piece = lax.dot_general(
            front[j * TILE :],
            held[j * TILE :, pl.ds(j * TILE, TILE)],
            (((0,), (0,)), ((), ())),
            preferred_element_type=jnp.float32,
        )
        out[pl.ds(j * TILE, TILE)] = piece.T


def local_solve(order, own, faces, factor):
    size, lanes = factor.shape[0], own.shape[-1]
    vmem = pl.BlockSpec(memory_space=pltpu.VMEM)
    return pl.pallas_call(
        local_kernel,
        out_shape=jax.ShapeDtypeStruct(own.shape, jnp.float32),
        in_specs=[vmem] * 8 + [pl.BlockSpec(memory_space=pl.ANY)],
        out_specs=vmem,
        scratch_shapes=[
            pltpu.VMEM((size, size), jnp.bfloat16),
            pltpu.VMEM((size, lanes), jnp.bfloat16),
            pltpu.VMEM((size, lanes), jnp.bfloat16),
            pltpu.VMEM((6 * faces[0].shape[0], lanes), jnp.bfloat16),
            pltpu.SemaphoreType.DMA((size // TILE,)),
        ],
        compiler_params=pltpu.CompilerParams(vmem_limit_bytes=24 * 1024 * 1024),
        name="local_solve",
    )(order, own, *faces, factor)


def spread(coarse_inverse):
    rows, total = coarse_inverse.shape
    count = lax.axis_size(X)
    width = total // count
    at_x, at_c = lax.axis_index(X), lax.axis_index(C)
    pieces = []
    for step in range(count):
        place = (at_x + step) % count
        piece = lax.dynamic_slice(coarse_inverse, (0, place * width), (rows, width))
        pieces.append(shift(piece, X, step) if step else piece)

    def half(core):
        start = (0, core * (width // 2))
        return jnp.concatenate(
            [lax.dynamic_slice(piece, start, (rows, width // 2)) for piece in pieces]
        )

    return half(at_c), shift(half(1 - at_c), C, 1)


def rolled(value, start, rows):
    doubled = jnp.concatenate([value, value])
    return lax.dynamic_slice(doubled, (start * rows, 0), value.shape)


def gathered(value):
    rows = value.shape[0]
    at_y, at_z = lax.axis_index(Y), lax.axis_index(Z)
    below, above = shift(value, Z, 1), shift(value, Z, -1)
    pair = jnp.concatenate([below, value])
    three = jnp.concatenate([pair, above])
    line = jnp.concatenate([shift(three, Z, 3), three, shift(pair, Z, -3)])
    line = rolled(line, (4 - at_z) % 8, rows)
    plane = jnp.concatenate([shift(line, Y, k) for k in (3, 2, 1)] + [line])
    return rolled(plane, 3 - at_y, line.shape[0])


def coarse_solve(stacks, whole, rows):
    mine, theirs = (
        jnp.dot(stack, whole, preferred_element_type=jnp.float32) for stack in stacks
    )
    mine = (mine + shift(theirs, C, 1)).reshape(-1, rows, whole.shape[-1])
    total = mine[0]
    for step in range(1, mine.shape[0]):
        total = total + shift(mine[step], X, -step)
    return total.astype(jnp.bfloat16)


def everywhere(partial):
    for axes in (GX, (Y, Z)):
        count = 1
        for axis in axes:
            count *= lax.axis_size(axis)
        copies = jnp.broadcast_to(partial[None], (count,) + partial.shape)
        partial = jnp.sum(lax.all_to_all(copies, axes, 0, 0, tiled=True), axis=0)
    return partial


def local(right_side, stiffness, local_factor, basis, coarse_map, margin_index, coarse_inverse):
    factor = local_factor.reshape(local_factor.shape[-2:])
    basis_count = basis.shape[-2]
    coarse_ids = coarse_map.reshape(-1)
    order = margin_index.reshape(-1, 1)
    placement = (
        coarse_ids[None, :] == lax.broadcasted_iota(jnp.int32, (basis_count, basis_count), 0)
    ).astype(jnp.bfloat16)
    functions = jnp.dot(
        placement, basis.reshape(basis.shape[-2:]), preferred_element_type=jnp.float32
    ).astype(jnp.bfloat16)
    contract_first = (((0,), (0,)), ((), ()))
    diagonal = 6.0 + stiffness[..., None]
    stacks = spread(coarse_inverse)

    def precondition(field):
        rounded = field.astype(jnp.bfloat16)
        own_rows = rounded.reshape(-1, rounded.shape[-1])
        placed = jnp.dot(functions, own_rows, preferred_element_type=jnp.float32).astype(
            jnp.bfloat16
        )
        whole = gathered(placed)
        local_part = local_solve(order, own_rows, halo(rounded), factor)
        whole, local_part = lax.optimization_barrier((whole, local_part))
        solved = coarse_solve(stacks, whole, basis_count)
        coarse_part = lax.dot_general(
            functions, solved, contract_first, preferred_element_type=jnp.float32
        )
        return (local_part + coarse_part).reshape(field.shape)

    def operate(field):
        faces = halo(field.astype(jnp.bfloat16))
        beside = None
        for dim in (1, 2, 3):
            shape = list(field.shape)
            shape[dim] = 1
            low, high = (
                face.astype(field.dtype).reshape(shape) for face in faces[2 * dim - 2 : 2 * dim]
            )
            length = field.shape[dim]
            before = jnp.concatenate([low, lax.slice_in_dim(field, 0, length - 1, axis=dim)], dim)
            after = jnp.concatenate([lax.slice_in_dim(field, 1, length, axis=dim), high], dim)
            beside = before + after if beside is None else beside + before + after
        return diagonal * field - beside

    raw = right_side * SCALE
    search_one = precondition(raw)
    image_one = operate(search_one)
    search_two = precondition(image_one)
    image_two = operate(search_two)
    gram = everywhere(
        jnp.stack(
            [
                inner(raw, raw),
                inner(image_one, raw),
                inner(image_one, image_one),
                inner(image_two, raw),
                inner(image_two, image_one),
                inner(image_two, image_two),
            ]
        )
    )
    weight_one, weight_two, ratio = weights(gram)
    return (weight_one * search_one + weight_two * search_two, ratio)


def solution(mesh):
    finer = Mesh(
        mesh.devices.reshape(4, 2, mesh.shape["gy"], mesh.shape["gz"]), ("gx_0", "gx_1", "gy", "gz")
    )
    placed = (
        P(None, GX, "gy", "gz", None),
        P(None, GX, "gy", "gz"),
        P(GX, "gy", "gz", None, None),
        P(GX, "gy", "gz", None, None),
        P(GX, "gy", "gz", None),
        P(GX, "gy", "gz", None),
        P(GX_GY_GZ, None),
    )
    return jax.shard_map(
        local,
        mesh=finer,
        in_specs=placed,
        out_specs=(P(None, GX, "gy", "gz", None), P()),
        check_vma=False,
    )
```

```python
import functools

import jax
import jax.numpy as jnp
from jax import lax
from jax.experimental import pallas as pl
from jax.experimental.pallas import tpu as pltpu
from jax.sharding import Mesh
from jax.sharding import PartitionSpec as P


X, C, Z = "gx_0", "gx_1", "gz"
GX, Y = (X, C), ("gy_0", "gy_1")
GX_GY_GZ = (*GX, *Y, Z)

EPSILON = 1e-06
SCALE = 2.0**-14
TILE = 256
SOME = 128


def shift(value, axis, step):
    count = lax.axis_size(axis)
    return lax.ppermute(value, axis, [(i, (i + step) % count) for i in range(count)])


def ends(blocks, dim):
    length, lanes = blocks.shape[dim], blocks.shape[-1]
    first = lax.slice_in_dim(blocks, 0, 1, axis=dim).reshape(-1, lanes)
    last = lax.slice_in_dim(blocks, length - 1, length, axis=dim).reshape(-1, lanes)
    return first, last


def swap_faces(blocks):
    first, last = ends(blocks, 1)
    lower = lax.axis_index(C) == 0
    inside = shift(jnp.where(lower, last, first), C, 1)
    peers = lax.axis_size(GX)
    up = [(i, i + 1) for i in range(1, peers - 1, 2)]
    across = lax.ppermute(
        jnp.where(lower, first, last), GX, up + [(b, a) for a, b in up]
    )
    return inside, across


def halo(blocks):
    inside, across = swap_faces(blocks)
    lower = lax.axis_index(C) == 0
    faces = [jnp.where(lower, across, inside), jnp.where(lower, inside, across)]
    for axis, dim in ((Y, 2), (Z, 3)):
        first, last = ends(blocks, dim)
        up = [(i, i + 1) for i in range(lax.axis_size(axis) - 1)]
        faces.append(lax.ppermute(last, axis, up))
        faces.append(lax.ppermute(first, axis, [(b, a) for a, b in up]))
    return faces


def inner(left, right):
    return jnp.sum(left * right, axis=(0, 1, 2, 3))


def weights(gram):
    raw_raw, one_raw, one_one, two_raw, two_one, two_two = (gram[i] for i in range(6))
    start_square = raw_raw / (SCALE * SCALE) + EPSILON
    start_norm = jnp.sqrt(start_square)
    size = start_norm * SCALE
    square = size * size
    kept = raw_raw / square
    along_one = one_raw / square
    rest_one = one_one / square - along_one * along_one * (2.0 - kept)
    rest_one = jnp.maximum(rest_one, 0.0) + EPSILON
    norm_two = jnp.sqrt(rest_one)
    kept_two = (rest_one - EPSILON) / rest_one
    shared = along_one * (1.0 - kept) / norm_two
    cross_two = (two_raw - along_one * one_raw) / (square * norm_two)
    along_two = (
        (two_one - along_one * two_raw) - along_one * (one_one - along_one * one_raw)
    ) / (square * rest_one)
    image_square = (two_two - along_one * (2.0 * two_one - along_one * one_one)) / (
        square * rest_one
    )
    rest_two = (
        image_square
        - cross_two * cross_two * (2.0 - kept)
        - along_two * along_two * (2.0 - kept_two)
        + 2.0 * cross_two * along_two * shared
    )
    norm_three = jnp.sqrt(jnp.maximum(rest_two, 0.0) + EPSILON)
    radius_one = jnp.sqrt(along_one * along_one + norm_two * norm_two)
    cosine_one = along_one / radius_one
    sine_one = norm_two / radius_one
    turned_one = cosine_one * cross_two + sine_one * along_two
    turned_two = cosine_one * along_two - sine_one * cross_two
    radius_two = jnp.sqrt(turned_two * turned_two + norm_three * norm_three)
    cosine_two = turned_two / radius_two
    sine_two = norm_three / radius_two
    coef_two = -cosine_two * sine_one * start_norm / radius_two
    coef_one = (cosine_one * start_norm - turned_one * coef_two) / radius_one
    weight_two = coef_two / (size * norm_two)
    weight_one = coef_one / size - along_one * weight_two
    return (weight_one, weight_two, sine_one * sine_two)


def local_kernel(place, order, own, *rest):
    faces, (factor, out, held, stacked, front, ring, done) = rest[:6], rest[6:]
    size = stacked.shape[0]
    own_count = own.shape[0]
    tiles = size // TILE
    half = size // 2

    def rows(i):
        return pl.ds(pl.multiple_of(i * TILE, TILE), TILE)

    def copy(i, width):
        return pltpu.make_async_copy(
            factor.at[rows(i), pl.ds(0, width)], held.at[rows(i), pl.ds(0, width)], done.at[i]
        )

    for i in range(tiles):
        copy(i, half if i < tiles // 2 else size).start()
    stacked[:own_count] = own[...]
    inside, across, y_low, y_high, z_low, z_high = faces
    per_part = inside.shape[0] // 3
    lower = place[0] == 0
    for part in range(3):

        def layer(face):
            skip = face.shape[0] - inside.shape[0]
            return face[pl.ds(skip + part * per_part, per_part)]

        def put(k, value):
            ring[pl.ds((part * 6 + k) * per_part, per_part)] = value

        put(0, jnp.where(lower, layer(across), layer(inside)))
        put(1, jnp.where(lower, layer(inside), layer(across)))
        for k, face in enumerate((y_low, y_high, z_low, z_high)):
            value = layer(face)
            put(2 + k, jnp.where(place[1 + k] != 0, value, jnp.zeros_like(value)))

    def pick(k):
        some = pl.ds(pl.multiple_of(k * SOME, SOME), SOME)
        table = lax.broadcasted_iota(jnp.int32, (SOME, ring.shape[0]), 1) == order[some]
        stacked[pl.ds(pl.multiple_of(own_count + k * SOME, SOME), SOME)] = jnp.dot(
            table.astype(jnp.float32).astype(jnp.bfloat16),
            ring[...],
            preferred_element_type=jnp.float32,
        ).astype(jnp.bfloat16)

    pl.loop(0, order.shape[0] // SOME)(pick)

    def ahead(width, i):
        copy(i, width).wait()
        front[rows(i)] = jnp.dot(
            held[rows(i), :width], stacked[:width], preferred_element_type=jnp.float32
        ).astype(jnp.bfloat16)

    def back(skip, j):
        piece = lax.dot_general(
            front[skip:], held[skip:, rows(j)], contract_first, preferred_element_type=jnp.float32
        )
        out[rows(j)] = piece.T

    contract_first = (((0,), (0,)), ((), ()))
    middle = tiles // 2
    pl.loop(0, middle)(functools.partial(ahead, half))
    pl.loop(middle, tiles)(functools.partial(ahead, size))
    pl.loop(0, middle)(functools.partial(back, 0))
    pl.loop(middle, own_count // TILE)(functools.partial(back, half))


def local_solve(place, order, own, faces, factor):
    size, lanes = factor.shape[0], own.shape[-1]
    vmem = pl.BlockSpec(memory_space=pltpu.VMEM)
    return pl.pallas_call(
        local_kernel,
        out_shape=jax.ShapeDtypeStruct(own.shape, jnp.float32),
        in_specs=[pl.BlockSpec(memory_space=pltpu.SMEM)]
        + [vmem] * 8
        + [pl.BlockSpec(memory_space=pltpu.HBM)],
        out_specs=vmem,
        scratch_shapes=[
            pltpu.VMEM((size, size), jnp.bfloat16),
            pltpu.VMEM((size, lanes), jnp.bfloat16),
            pltpu.VMEM((size, lanes), jnp.bfloat16),
            pltpu.VMEM((6 * faces[0].shape[0], lanes), jnp.bfloat16),
            pltpu.SemaphoreType.DMA((size // TILE,)),
        ],
        compiler_params=pltpu.CompilerParams(vmem_limit_bytes=24 * 1024 * 1024),
        name="local_solve",
    )(place, order, own, *faces, factor)


def stack_kernel(place, *refs):
    pieces, (mine, theirs) = refs[:-2], refs[-2:]
    rows, width = pieces[0].shape[0], mine.shape[1]
    for core, out in ((place[1], mine), (1 - place[1], theirs)):
        columns = pl.ds(pl.multiple_of(core * width, width), width)
        for step, piece in enumerate(pieces):
            out[pl.ds(step * rows, rows)] = piece[:, columns]


def stack(coarse_inverse, pieces):
    rows, width = pieces[0].shape
    count = len(pieces) + 1
    place = jnp.stack([lax.axis_index(X), lax.axis_index(C)]).astype(jnp.int32)
    whole = pl.BlockSpec((rows, width), lambda i, place: (0, 0))
    result = pl.BlockSpec((rows * count, width // 2), lambda i, place: (0, 0))
    shape = jax.ShapeDtypeStruct((rows * count, width // 2), coarse_inverse.dtype)
    return pl.pallas_call(
        stack_kernel,
        out_shape=(shape, shape),
        grid_spec=pltpu.PrefetchScalarGridSpec(
            num_scalar_prefetch=1,
            grid=(1,),
            in_specs=[pl.BlockSpec((rows, width), lambda i, place: (0, place[0]))]
            + [whole] * len(pieces),
            out_specs=(result, result),
        ),
        name="stack",
    )(place, coarse_inverse, *pieces)


def spread(coarse_inverse):
    rows, total = coarse_inverse.shape
    count = lax.axis_size(X)
    width = total // count
    at_x = lax.axis_index(X)
    pieces = []
    for step in range(1, count):
        place = (at_x + step) & (count - 1)
        piece = lax.dynamic_slice(coarse_inverse, (0, place * width), (rows, width))
        pieces.append(shift(piece, X, step))
    return stack(coarse_inverse, pieces)


def rolled(value, start, rows):
    doubled = jnp.concatenate([value, value])
    return lax.dynamic_slice(doubled, (start * rows, 0), value.shape)


def gathered(value, blocks):
    rows = value.shape[0]
    at_y, at_z = lax.axis_index(Y), lax.axis_index(Z)
    first, last = ends(blocks, 3)
    z_low = shift(jnp.concatenate([value, last]), Z, 1)
    z_high = shift(jnp.concatenate([value, first]), Z, -1)
    inside, across = swap_faces(blocks)
    pair = jnp.concatenate([z_low[:rows], value])
    three = jnp.concatenate([pair, z_high[:rows]])
    line = jnp.concatenate([shift(three, Z, 3), three, shift(pair, Z, -3)])
    line = rolled(line, (12 - at_z) & 7, rows)
    count = line.shape[0]
    first, last = ends(blocks, 2)
    opposite = shift(line, Y, 2)
    y_low = shift(jnp.concatenate([line, last]), Y, 1)
    y_high = shift(jnp.concatenate([line, first]), Y, 3)
    plane = jnp.concatenate([y_high[:count], opposite, y_low[:count], line])
    return rolled(plane, 3 - at_y, count), (inside, across, y_low, y_high, z_low, z_high)


def coarse_solve(stacks, whole, rows):
    theirs = shift(whole, C, 1)
    parts = jnp.dot(stacks[0], whole, preferred_element_type=jnp.float32)
    parts = parts + jnp.dot(stacks[1], theirs, preferred_element_type=jnp.float32)
    total = parts[:rows]
    for step in range(1, parts.shape[0] // rows):
        part = parts[step * rows : (step + 1) * rows]
        total = total + shift(part, X, -step)
    return total.astype(jnp.bfloat16)


def everywhere(partial):
    for axes in ((*GX, Y[1]), (Y[0], Z)):
        count = 1
        for axis in axes:
            count *= lax.axis_size(axis)
        copies = jnp.broadcast_to(partial[None], (count,) + partial.shape)
        partial = jnp.sum(lax.all_to_all(copies, axes, 0, 0, tiled=True), axis=0)
    return partial


def local(right_side, stiffness, local_factor, basis, coarse_map, margin_index, coarse_inverse):
    factor = local_factor.reshape(local_factor.shape[-2:])
    basis_count = basis.shape[-2]
    coarse_ids = coarse_map.reshape(-1)
    order = margin_index.reshape(-1, 1)
    placement = (
        coarse_ids[None, :] == lax.broadcasted_iota(jnp.int32, (basis_count, basis_count), 0)
    ).astype(jnp.bfloat16)
    functions = jnp.dot(
        placement, basis.reshape(basis.shape[-2:]), preferred_element_type=jnp.float32
    ).astype(jnp.bfloat16)
    contract_first = (((0,), (0,)), ((), ()))
    at_y, at_z = lax.axis_index(Y), lax.axis_index(Z)
    place = jnp.stack(
        [
            lax.axis_index(C),
            at_y > 0,
            at_y < lax.axis_size(Y) - 1,
            at_z > 0,
            at_z < lax.axis_size(Z) - 1,
        ]
    ).astype(jnp.int32)
    diagonal = 6.0 + stiffness[..., None]
    stacks = spread(coarse_inverse)

    def precondition(field):
        rounded = field.astype(jnp.bfloat16)
        own_rows = rounded.reshape(-1, rounded.shape[-1])
        placed = jnp.dot(functions, own_rows, preferred_element_type=jnp.float32).astype(
            jnp.bfloat16
        )
        whole, faces = gathered(placed, rounded)
        local_part = local_solve(place, order, own_rows, faces, factor)
        solved = coarse_solve(stacks, whole, basis_count)
        coarse_part = lax.dot_general(
            functions, solved, contract_first, preferred_element_type=jnp.float32
        )
        return (local_part + coarse_part).reshape(field.shape)

    def operate(field):
        faces = halo(field.astype(jnp.bfloat16))
        beside = None
        for dim in (1, 2, 3):
            shape = list(field.shape)
            shape[dim] = 1
            low, high = (
                face.astype(field.dtype).reshape(shape) for face in faces[2 * dim - 2 : 2 * dim]
            )
            length = field.shape[dim]
            before = jnp.concatenate([low, lax.slice_in_dim(field, 0, length - 1, axis=dim)], dim)
            after = jnp.concatenate([lax.slice_in_dim(field, 1, length, axis=dim), high], dim)
            beside = before + after if beside is None else beside + before + after
        return diagonal * field - beside

    raw = right_side * SCALE
    search_one = precondition(raw)
    image_one = operate(search_one)
    search_two = precondition(image_one)
    image_two = operate(search_two)
    gram = everywhere(
        jnp.stack(
            [
                inner(raw, raw),
                inner(image_one, raw),
                inner(image_one, image_one),
                inner(image_two, raw),
                inner(image_two, image_one),
                inner(image_two, image_two),
            ]
        )
    )
    weight_one, weight_two, ratio = weights(gram)
    return (weight_one * search_one + weight_two * search_two, ratio)


def solution(mesh):
    finer = Mesh(
        mesh.devices.reshape(4, 2, 2, 2, mesh.shape["gz"]), ("gx_0", "gx_1", "gy_0", "gy_1", "gz")
    )
    placed = (
        P(None, GX, Y, Z, None),
        P(None, GX, Y, Z),
        P(GX, Y, Z, None, None),
        P(GX, Y, Z, None, None),
        P(GX, Y, Z, None),
        P(GX, Y, Z, None),
        P(GX_GY_GZ, None),
    )
    return jax.shard_map(
        local,
        mesh=finer,
        in_specs=placed,
        out_specs=(P(None, GX, Y, Z, None), P()),
        check_vma=False,
    )
```

```python
import jax
import jax.numpy as jnp
from jax import lax
from jax.experimental import pallas as pl
from jax.experimental.pallas import tpu as pltpu
from jax.sharding import Mesh
from jax.sharding import PartitionSpec as P


X, C, Z = "gx_0", "gx_1", "gz"
GX, Y = (X, C), ("gy_0", "gy_1")
GX_GY_GZ = (*GX, *Y, Z)

EPSILON = 1e-06
SCALE = 2.0**-14
TILE = 256
SOME = 128


def shift(value, axis, step):
    count = lax.axis_size(axis)
    return lax.ppermute(value, axis, [(i, (i + step) % count) for i in range(count)])


def ends(blocks, dim):
    length, lanes = blocks.shape[dim], blocks.shape[-1]
    first = lax.slice_in_dim(blocks, 0, 1, axis=dim).reshape(-1, lanes)
    last = lax.slice_in_dim(blocks, length - 1, length, axis=dim).reshape(-1, lanes)
    return first, last


def swap_faces(blocks):
    first, last = ends(blocks, 1)
    lower = lax.axis_index(C) == 0
    inside = shift(jnp.where(lower, last, first), C, 1)
    peers = lax.axis_size(GX)
    up = [(i, i + 1) for i in range(1, peers - 1, 2)]
    across = lax.ppermute(
        jnp.where(lower, first, last), GX, up + [(b, a) for a, b in up]
    )
    return inside, across


def halo(blocks):
    inside, across = swap_faces(blocks)
    lower = lax.axis_index(C) == 0
    faces = [jnp.where(lower, across, inside), jnp.where(lower, inside, across)]
    for axis, dim in ((Y, 2), (Z, 3)):
        first, last = ends(blocks, dim)
        up = [(i, i + 1) for i in range(lax.axis_size(axis) - 1)]
        faces.append(lax.ppermute(last, axis, up))
        faces.append(lax.ppermute(first, axis, [(b, a) for a, b in up]))
    return faces


def inner(left, right):
    return jnp.sum(left * right, axis=(0, 1, 2, 3))


def weights(gram):
    raw_raw, one_raw, one_one, two_raw, two_one, two_two = (gram[i] for i in range(6))
    start_square = raw_raw / (SCALE * SCALE) + EPSILON
    start_norm = jnp.sqrt(start_square)
    size = start_norm * SCALE
    square = size * size
    kept = raw_raw / square
    along_one = one_raw / square
    rest_one = one_one / square - along_one * along_one * (2.0 - kept)
    rest_one = jnp.maximum(rest_one, 0.0) + EPSILON
    norm_two = jnp.sqrt(rest_one)
    kept_two = (rest_one - EPSILON) / rest_one
    shared = along_one * (1.0 - kept) / norm_two
    cross_two = (two_raw - along_one * one_raw) / (square * norm_two)
    along_two = (
        (two_one - along_one * two_raw) - along_one * (one_one - along_one * one_raw)
    ) / (square * rest_one)
    image_square = (two_two - along_one * (2.0 * two_one - along_one * one_one)) / (
        square * rest_one
    )
    rest_two = (
        image_square
        - cross_two * cross_two * (2.0 - kept)
        - along_two * along_two * (2.0 - kept_two)
        + 2.0 * cross_two * along_two * shared
    )
    norm_three = jnp.sqrt(jnp.maximum(rest_two, 0.0) + EPSILON)
    radius_one = jnp.sqrt(along_one * along_one + norm_two * norm_two)
    cosine_one = along_one / radius_one
    sine_one = norm_two / radius_one
    turned_one = cosine_one * cross_two + sine_one * along_two
    turned_two = cosine_one * along_two - sine_one * cross_two
    radius_two = jnp.sqrt(turned_two * turned_two + norm_three * norm_three)
    cosine_two = turned_two / radius_two
    sine_two = norm_three / radius_two
    coef_two = -cosine_two * sine_one * start_norm / radius_two
    coef_one = (cosine_one * start_norm - turned_one * coef_two) / radius_one
    weight_two = coef_two / (size * norm_two)
    weight_one = coef_one / size - along_one * weight_two
    return (weight_one, weight_two, sine_one * sine_two)


def local_kernel(place, order, own, *rest):
    faces, (factor, out, held, stacked, front, ring, done) = rest[:6], rest[6:]
    size = stacked.shape[0]
    own_count = own.shape[0]
    tiles = size // TILE

    def copy(i):
        rows, width = pl.ds(i * TILE, TILE), (i + 1) * TILE
        return pltpu.make_async_copy(
            factor.at[rows, pl.ds(0, width)], held.at[rows, pl.ds(0, width)], done.at[i]
        )

    for i in range(tiles):
        copy(i).start()
    stacked[:own_count] = own[...]
    inside, across, y_low, y_high, z_low, z_high = faces
    per_part = inside.shape[0] // 3
    lower = place[0] == 0
    for part in range(3):

        def layer(face):
            skip = face.shape[0] - inside.shape[0]
            return face[pl.ds(skip + part * per_part, per_part)]

        def put(k, value):
            ring[pl.ds((part * 6 + k) * per_part, per_part)] = value

        put(0, jnp.where(lower, layer(across), layer(inside)))
        put(1, jnp.where(lower, layer(inside), layer(across)))
        for k, face in enumerate((y_low, y_high, z_low, z_high)):
            value = layer(face)
            put(2 + k, jnp.where(place[1 + k] != 0, value, jnp.zeros_like(value)))

    def pick(k):
        some = pl.ds(pl.multiple_of(k * SOME, SOME), SOME)
        table = lax.broadcasted_iota(jnp.int32, (SOME, ring.shape[0]), 1) == order[some]
        stacked[pl.ds(pl.multiple_of(own_count + k * SOME, SOME), SOME)] = jnp.dot(
            table.astype(jnp.float32).astype(jnp.bfloat16),
            ring[...],
            preferred_element_type=jnp.float32,
        ).astype(jnp.bfloat16)

    pl.loop(0, order.shape[0] // SOME)(pick)

    for i in range(tiles):
        copy(i).wait()
        rows, width = pl.ds(i * TILE, TILE), (i + 1) * TILE
        front[rows] = jnp.dot(
            held[rows, :width], stacked[:width], preferred_element_type=jnp.float32
        ).astype(jnp.bfloat16)
    for j in range(own_count // TILE):
        rows = pl.ds(j * TILE, TILE)
        piece = lax.dot_general(
            front[j * TILE :],
            held[j * TILE :, rows],
            (((0,), (0,)), ((), ())),
            preferred_element_type=jnp.float32,
        )
        out[rows] = piece.T


def local_solve(place, order, own, faces, factor):
    size, lanes = factor.shape[0], own.shape[-1]
    vmem = pl.BlockSpec(memory_space=pltpu.VMEM)
    return pl.pallas_call(
        local_kernel,
        out_shape=jax.ShapeDtypeStruct(own.shape, jnp.float32),
        in_specs=[pl.BlockSpec(memory_space=pltpu.SMEM)]
        + [vmem] * 8
        + [pl.BlockSpec(memory_space=pltpu.HBM)],
        out_specs=vmem,
        scratch_shapes=[
            pltpu.VMEM((size, size), jnp.bfloat16),
            pltpu.VMEM((size, lanes), jnp.bfloat16),
            pltpu.VMEM((size, lanes), jnp.bfloat16),
            pltpu.VMEM((6 * faces[0].shape[0], lanes), jnp.bfloat16),
            pltpu.SemaphoreType.DMA((size // TILE,)),
        ],
        compiler_params=pltpu.CompilerParams(vmem_limit_bytes=57 * 1024 * 1024),
        name="local_solve",
    )(place, order, own, *faces, factor)


def stack_kernel(place, *refs):
    pieces, (mine, theirs) = refs[:-2], refs[-2:]
    rows, width = pieces[0].shape[0], mine.shape[1]
    for core, out in ((place[0], mine), (1 - place[0], theirs)):
        columns = pl.ds(pl.multiple_of(core * width, width), width)
        for step, piece in enumerate(pieces):
            out[pl.ds(step * rows, rows)] = piece[:, columns]


def stack(place, pieces):
    rows, width = pieces[0].shape
    vmem = pl.BlockSpec(memory_space=pltpu.VMEM)
    shape = jax.ShapeDtypeStruct((rows * len(pieces), width // 2), pieces[0].dtype)
    return pl.pallas_call(
        stack_kernel,
        out_shape=(shape, shape),
        in_specs=[pl.BlockSpec(memory_space=pltpu.SMEM)] + [vmem] * len(pieces),
        out_specs=(vmem, vmem),
        compiler_params=pltpu.CompilerParams(vmem_limit_bytes=6 * 1024 * 1024),
        name="stack",
    )(place, *pieces)


def spread(place, coarse_inverse):
    rows, total = coarse_inverse.shape
    count = lax.axis_size(X)
    width = total // count
    at_x = lax.axis_index(X)
    pieces = []
    for step in range(count):
        at = (at_x + step) & (count - 1)
        piece = lax.dynamic_slice(coarse_inverse, (0, at * width), (rows, width))
        pieces.append(shift(piece, X, step) if step else piece)
    return stack(place, pieces)


def rolled(value, start, rows):
    doubled = jnp.concatenate([value, value])
    return lax.dynamic_slice(doubled, (start * rows, 0), value.shape)


def gathered(value, blocks):
    rows = value.shape[0]
    at_y, at_z = lax.axis_index(Y), lax.axis_index(Z)
    first, last = ends(blocks, 3)
    z_low = shift(jnp.concatenate([value, last]), Z, 1)
    z_high = shift(jnp.concatenate([value, first]), Z, -1)
    inside, across = swap_faces(blocks)
    pair = jnp.concatenate([z_low[:rows], value])
    three = jnp.concatenate([pair, z_high[:rows]])
    line = jnp.concatenate([shift(three, Z, 3), three, shift(pair, Z, -3)])
    line = rolled(line, (12 - at_z) & 7, rows)
    count = line.shape[0]
    first, last = ends(blocks, 2)
    opposite = shift(line, Y, 2)
    y_low = shift(jnp.concatenate([line, last]), Y, 1)
    y_high = shift(jnp.concatenate([line, first]), Y, 3)
    plane = jnp.concatenate([y_high[:count], opposite, y_low[:count], line])
    return rolled(plane, 3 - at_y, count), (inside, across, y_low, y_high, z_low, z_high)


def coarse_solve(stacks, whole, rows):
    theirs = shift(whole, C, 1)
    parts = jnp.dot(stacks[0], whole, preferred_element_type=jnp.float32)
    parts = parts + jnp.dot(stacks[1], theirs, preferred_element_type=jnp.float32)
    total = parts[:rows]
    for step in range(1, parts.shape[0] // rows):
        part = parts[step * rows : (step + 1) * rows]
        total = total + shift(part, X, -step)
    return total.astype(jnp.bfloat16)


def everywhere(partial):
    for axes in ((*GX, Y[1]), (Y[0], Z)):
        count = 1
        for axis in axes:
            count *= lax.axis_size(axis)
        copies = jnp.broadcast_to(partial[None], (count,) + partial.shape)
        partial = jnp.sum(lax.all_to_all(copies, axes, 0, 0, tiled=True), axis=0)
    return partial


def local(right_side, stiffness, local_factor, basis, coarse_map, margin_index, coarse_inverse):
    factor = local_factor.reshape(local_factor.shape[-2:])
    basis_count = basis.shape[-2]
    coarse_ids = coarse_map.reshape(-1)
    order = margin_index.reshape(-1, 1)
    placement = (
        coarse_ids[None, :] == lax.broadcasted_iota(jnp.int32, (basis_count, basis_count), 0)
    ).astype(jnp.bfloat16)
    functions = jnp.dot(
        placement, basis.reshape(basis.shape[-2:]), preferred_element_type=jnp.float32
    ).astype(jnp.bfloat16)
    contract_first = (((0,), (0,)), ((), ()))
    at_y, at_z = lax.axis_index(Y), lax.axis_index(Z)
    place = jnp.stack(
        [
            lax.axis_index(C),
            at_y > 0,
            at_y < lax.axis_size(Y) - 1,
            at_z > 0,
            at_z < lax.axis_size(Z) - 1,
        ]
    ).astype(jnp.int32)
    stacks = spread(place, coarse_inverse)
    diagonal = 6.0 + stiffness[..., None]

    def precondition(field):
        rounded = field.astype(jnp.bfloat16)
        own_rows = rounded.reshape(-1, rounded.shape[-1])
        placed = jnp.dot(functions, own_rows, preferred_element_type=jnp.float32).astype(
            jnp.bfloat16
        )
        whole, faces = gathered(placed, rounded)
        local_part = local_solve(place, order, own_rows, faces, factor)
        solved = coarse_solve(stacks, whole, basis_count)
        coarse_part = lax.dot_general(
            functions, solved, contract_first, preferred_element_type=jnp.float32
        )
        return (local_part + coarse_part).reshape(field.shape)

    def operate(field):
        faces = halo(field.astype(jnp.bfloat16))
        beside = None
        for dim in (1, 2, 3):
            shape = list(field.shape)
            shape[dim] = 1
            low, high = (
                face.astype(field.dtype).reshape(shape) for face in faces[2 * dim - 2 : 2 * dim]
            )
            length = field.shape[dim]
            before = jnp.concatenate([low, lax.slice_in_dim(field, 0, length - 1, axis=dim)], dim)
            after = jnp.concatenate([lax.slice_in_dim(field, 1, length, axis=dim), high], dim)
            beside = before + after if beside is None else beside + before + after
        return diagonal * field - beside

    raw = right_side * SCALE
    search_one = precondition(raw)
    image_one = operate(search_one)
    search_two = precondition(image_one)
    image_two = operate(search_two)
    gram = everywhere(
        jnp.stack(
            [
                inner(raw, raw),
                inner(image_one, raw),
                inner(image_one, image_one),
                inner(image_two, raw),
                inner(image_two, image_one),
                inner(image_two, image_two),
            ]
        )
    )
    weight_one, weight_two, ratio = weights(gram)
    return (weight_one * search_one + weight_two * search_two, ratio)


def solution(mesh):
    finer = Mesh(
        mesh.devices.reshape(4, 2, 2, 2, mesh.shape["gz"]), ("gx_0", "gx_1", "gy_0", "gy_1", "gz")
    )
    placed = (
        P(None, GX, Y, Z, None),
        P(None, GX, Y, Z),
        P(GX, Y, Z, None, None),
        P(GX, Y, Z, None, None),
        P(GX, Y, Z, None),
        P(GX, Y, Z, None),
        P(GX_GY_GZ, None),
    )
    return jax.shard_map(
        local,
        mesh=finer,
        in_specs=placed,
        out_specs=(P(None, GX, Y, Z, None), P()),
        check_vma=False,
    )
```

```python
import functools

import jax
import jax.numpy as jnp
from jax import lax
from jax.experimental import pallas as pl
from jax.experimental.pallas import tpu as pltpu
from jax.sharding import Mesh
from jax.sharding import PartitionSpec as P


X, C, Z = "gx_0", "gx_1", "gz"
GX, Y = (X, C), ("gy_0", "gy_1")
GX_GY_GZ = (*GX, *Y, Z)

EPSILON = 1e-06
SCALE = 2.0**-14
TILE = 256
SOME = 128


def shift(value, axis, step):
    count = lax.axis_size(axis)
    return lax.ppermute(value, axis, [(i, (i + step) % count) for i in range(count)])


def ends(blocks, dim):
    length, lanes = blocks.shape[dim], blocks.shape[-1]
    first = lax.slice_in_dim(blocks, 0, 1, axis=dim).reshape(-1, lanes)
    last = lax.slice_in_dim(blocks, length - 1, length, axis=dim).reshape(-1, lanes)
    return first, last


def swap_faces(blocks):
    first, last = ends(blocks, 1)
    lower = lax.axis_index(C) == 0
    inside = shift(jnp.where(lower, last, first), C, 1)
    peers = lax.axis_size(GX)
    up = [(i, i + 1) for i in range(1, peers - 1, 2)]
    across = lax.ppermute(
        jnp.where(lower, first, last), GX, up + [(b, a) for a, b in up]
    )
    return inside, across


def halo(blocks):
    inside, across = swap_faces(blocks)
    lower = lax.axis_index(C) == 0
    faces = [jnp.where(lower, across, inside), jnp.where(lower, inside, across)]
    for axis, dim in ((Y, 2), (Z, 3)):
        first, last = ends(blocks, dim)
        up = [(i, i + 1) for i in range(lax.axis_size(axis) - 1)]
        faces.append(lax.ppermute(last, axis, up))
        faces.append(lax.ppermute(first, axis, [(b, a) for a, b in up]))
    return faces


def inner(left, right):
    return jnp.sum(left * right, axis=(0, 1, 2, 3))


def weights(gram):
    raw_raw, one_raw, one_one, two_raw, two_one, two_two = (gram[i] for i in range(6))
    start_square = raw_raw / (SCALE * SCALE) + EPSILON
    start_norm = jnp.sqrt(start_square)
    size = start_norm * SCALE
    square = size * size
    kept = raw_raw / square
    along_one = one_raw / square
    rest_one = one_one / square - along_one * along_one * (2.0 - kept)
    rest_one = jnp.maximum(rest_one, 0.0) + EPSILON
    norm_two = jnp.sqrt(rest_one)
    kept_two = (rest_one - EPSILON) / rest_one
    shared = along_one * (1.0 - kept) / norm_two
    cross_two = (two_raw - along_one * one_raw) / (square * norm_two)
    along_two = (
        (two_one - along_one * two_raw) - along_one * (one_one - along_one * one_raw)
    ) / (square * rest_one)
    image_square = (two_two - along_one * (2.0 * two_one - along_one * one_one)) / (
        square * rest_one
    )
    rest_two = (
        image_square
        - cross_two * cross_two * (2.0 - kept)
        - along_two * along_two * (2.0 - kept_two)
        + 2.0 * cross_two * along_two * shared
    )
    norm_three = jnp.sqrt(jnp.maximum(rest_two, 0.0) + EPSILON)
    radius_one = jnp.sqrt(along_one * along_one + norm_two * norm_two)
    cosine_one = along_one / radius_one
    sine_one = norm_two / radius_one
    turned_one = cosine_one * cross_two + sine_one * along_two
    turned_two = cosine_one * along_two - sine_one * cross_two
    radius_two = jnp.sqrt(turned_two * turned_two + norm_three * norm_three)
    cosine_two = turned_two / radius_two
    sine_two = norm_three / radius_two
    coef_two = -cosine_two * sine_one * start_norm / radius_two
    coef_one = (cosine_one * start_norm - turned_one * coef_two) / radius_one
    weight_two = coef_two / (size * norm_two)
    weight_one = coef_one / size - along_one * weight_two
    return (weight_one, weight_two, sine_one * sine_two)


def local_kernel(place, order, own, *rest):
    faces, (factor, out, held, stacked, front, ring, done) = rest[:6], rest[6:]
    size = stacked.shape[0]
    own_count = own.shape[0]
    tiles = size // TILE
    half = size // 2

    def rows(i):
        return pl.ds(pl.multiple_of(i * TILE, TILE), TILE)

    def copy(i, width):
        return pltpu.make_async_copy(
            factor.at[rows(i), pl.ds(0, width)], held.at[rows(i), pl.ds(0, width)], done.at[i]
        )

    for i in range(tiles):
        copy(i, half if i < tiles // 2 else size).start()
    stacked[:own_count] = own[...]
    inside, across, y_low, y_high, z_low, z_high = faces
    per_part = inside.shape[0] // 3
    lower = place[0] == 0
    for part in range(3):

        def layer(face):
            skip = face.shape[0] - inside.shape[0]
            return face[pl.ds(skip + part * per_part, per_part)]

        def put(k, value):
            ring[pl.ds((part * 6 + k) * per_part, per_part)] = value

        put(0, jnp.where(lower, layer(across), layer(inside)))
        put(1, jnp.where(lower, layer(inside), layer(across)))
        for k, face in enumerate((y_low, y_high, z_low, z_high)):
            value = layer(face)
            put(2 + k, jnp.where(place[1 + k] != 0, value, jnp.zeros_like(value)))

    def pick(k):
        some = pl.ds(pl.multiple_of(k * SOME, SOME), SOME)
        table = lax.broadcasted_iota(jnp.int32, (SOME, ring.shape[0]), 1) == order[some]
        stacked[pl.ds(pl.multiple_of(own_count + k * SOME, SOME), SOME)] = jnp.dot(
            table.astype(jnp.float32).astype(jnp.bfloat16),
            ring[...],
            preferred_element_type=jnp.float32,
        ).astype(jnp.bfloat16)

    pl.loop(0, order.shape[0] // SOME)(pick)

    def ahead(width, i):
        copy(i, width).wait()
        front[rows(i)] = jnp.dot(
            held[rows(i), :width], stacked[:width], preferred_element_type=jnp.float32
        ).astype(jnp.bfloat16)

    def back(skip, j):
        piece = lax.dot_general(
            front[skip:], held[skip:, rows(j)], contract_first, preferred_element_type=jnp.float32
        )
        out[rows(j)] = piece.T

    contract_first = (((0,), (0,)), ((), ()))
    middle = tiles // 2
    pl.loop(0, middle)(functools.partial(ahead, half))
    pl.loop(middle, tiles)(functools.partial(ahead, size))
    pl.loop(0, middle)(functools.partial(back, 0))
    pl.loop(middle, own_count // TILE)(functools.partial(back, half))


def local_solve(place, order, own, faces, factor):
    size, lanes = factor.shape[0], own.shape[-1]
    vmem = pl.BlockSpec(memory_space=pltpu.VMEM)
    return pl.pallas_call(
        local_kernel,
        out_shape=jax.ShapeDtypeStruct(own.shape, jnp.float32),
        in_specs=[pl.BlockSpec(memory_space=pltpu.SMEM)]
        + [vmem] * 8
        + [pl.BlockSpec(memory_space=pltpu.HBM)],
        out_specs=vmem,
        scratch_shapes=[
            pltpu.VMEM((size, size), jnp.bfloat16),
            pltpu.VMEM((size, lanes), jnp.bfloat16),
            pltpu.VMEM((size, lanes), jnp.bfloat16),
            pltpu.VMEM((6 * faces[0].shape[0], lanes), jnp.bfloat16),
            pltpu.SemaphoreType.DMA((size // TILE,)),
        ],
        compiler_params=pltpu.CompilerParams(vmem_limit_bytes=24 * 1024 * 1024),
        name="local_solve",
    )(place, order, own, *faces, factor)


def stack_kernel(place, *refs):
    pieces, (mine, theirs) = refs[:-2], refs[-2:]
    rows, width = pieces[0].shape[0], mine.shape[1]
    for core, out in ((place[0], mine), (1 - place[0], theirs)):
        columns = pl.ds(pl.multiple_of(core * width, width), width)
        for step, piece in enumerate(pieces):
            out[pl.ds(step * rows, rows)] = piece[:, columns]


def stack(place, pieces):
    rows, width = pieces[0].shape
    vmem = pl.BlockSpec(memory_space=pltpu.VMEM)
    shape = jax.ShapeDtypeStruct((rows * len(pieces), width // 2), pieces[0].dtype)
    return pl.pallas_call(
        stack_kernel,
        out_shape=(shape, shape),
        in_specs=[pl.BlockSpec(memory_space=pltpu.SMEM)] + [vmem] * len(pieces),
        out_specs=(vmem, vmem),
        compiler_params=pltpu.CompilerParams(vmem_limit_bytes=6 * 1024 * 1024),
        name="stack",
    )(place, *pieces)


def spread(place, coarse_inverse):
    rows, total = coarse_inverse.shape
    count = lax.axis_size(X)
    width = total // count
    at_x = lax.axis_index(X)
    pieces = []
    for step in range(count):
        at = (at_x + step) & (count - 1)
        piece = lax.dynamic_slice(coarse_inverse, (0, at * width), (rows, width))
        pieces.append(shift(piece, X, step) if step else piece)
    return stack(place, pieces)


def rolled(value, start, rows):
    doubled = jnp.concatenate([value, value])
    return lax.dynamic_slice(doubled, (start * rows, 0), value.shape)


def gathered(value, blocks):
    rows = value.shape[0]
    at_y, at_z = lax.axis_index(Y), lax.axis_index(Z)
    first, last = ends(blocks, 3)
    z_low = shift(jnp.concatenate([value, last]), Z, 1)
    z_high = shift(jnp.concatenate([value, first]), Z, -1)
    inside, across = swap_faces(blocks)
    pair = jnp.concatenate([z_low[:rows], value])
    three = jnp.concatenate([pair, z_high[:rows]])
    line = jnp.concatenate([shift(three, Z, 3), three, shift(pair, Z, -3)])
    line = rolled(line, (12 - at_z) & 7, rows)
    count = line.shape[0]
    first, last = ends(blocks, 2)
    opposite = shift(line, Y, 2)
    y_low = shift(jnp.concatenate([line, last]), Y, 1)
    y_high = shift(jnp.concatenate([line, first]), Y, 3)
    plane = jnp.concatenate([y_high[:count], opposite, y_low[:count], line])
    return rolled(plane, 3 - at_y, count), (inside, across, y_low, y_high, z_low, z_high)


def coarse_solve(stacks, whole, rows):
    theirs = shift(whole, C, 1)
    parts = jnp.dot(stacks[0], whole, preferred_element_type=jnp.float32)
    parts = parts + jnp.dot(stacks[1], theirs, preferred_element_type=jnp.float32)
    total = parts[:rows]
    for step in range(1, parts.shape[0] // rows):
        part = parts[step * rows : (step + 1) * rows]
        total = total + shift(part, X, -step)
    return total.astype(jnp.bfloat16)


def everywhere(partial):
    for axes in ((*GX, Y[1]), (Y[0], Z)):
        count = 1
        for axis in axes:
            count *= lax.axis_size(axis)
        copies = jnp.broadcast_to(partial[None], (count,) + partial.shape)
        partial = jnp.sum(lax.all_to_all(copies, axes, 0, 0, tiled=True), axis=0)
    return partial


def local(right_side, stiffness, local_factor, basis, coarse_map, margin_index, coarse_inverse):
    factor = local_factor.reshape(local_factor.shape[-2:])
    basis_count = basis.shape[-2]
    coarse_ids = coarse_map.reshape(-1)
    order = margin_index.reshape(-1, 1)
    placement = (
        coarse_ids[None, :] == lax.broadcasted_iota(jnp.int32, (basis_count, basis_count), 0)
    ).astype(jnp.bfloat16)
    functions = jnp.dot(
        placement, basis.reshape(basis.shape[-2:]), preferred_element_type=jnp.float32
    ).astype(jnp.bfloat16)
    contract_first = (((0,), (0,)), ((), ()))
    at_y, at_z = lax.axis_index(Y), lax.axis_index(Z)
    place = jnp.stack(
        [
            lax.axis_index(C),
            at_y > 0,
            at_y < lax.axis_size(Y) - 1,
            at_z > 0,
            at_z < lax.axis_size(Z) - 1,
        ]
    ).astype(jnp.int32)
    stacks = spread(place, coarse_inverse)
    diagonal = 6.0 + stiffness[..., None]

    def precondition(field):
        rounded = field.astype(jnp.bfloat16)
        own_rows = rounded.reshape(-1, rounded.shape[-1])
        placed = jnp.dot(functions, own_rows, preferred_element_type=jnp.float32).astype(
            jnp.bfloat16
        )
        whole, faces = gathered(placed, rounded)
        local_part = local_solve(place, order, own_rows, faces, factor)
        solved = coarse_solve(stacks, whole, basis_count)
        coarse_part = lax.dot_general(
            functions, solved, contract_first, preferred_element_type=jnp.float32
        )
        return (local_part + coarse_part).reshape(field.shape)

    def operate(field):
        faces = halo(field.astype(jnp.bfloat16))
        beside = None
        for dim in (1, 2, 3):
            shape = list(field.shape)
            shape[dim] = 1
            low, high = (
                face.astype(field.dtype).reshape(shape) for face in faces[2 * dim - 2 : 2 * dim]
            )
            length = field.shape[dim]
            before = jnp.concatenate([low, lax.slice_in_dim(field, 0, length - 1, axis=dim)], dim)
            after = jnp.concatenate([lax.slice_in_dim(field, 1, length, axis=dim), high], dim)
            beside = before + after if beside is None else beside + before + after
        return diagonal * field - beside

    raw = right_side * SCALE
    search_one = precondition(raw)
    image_one = operate(search_one)
    search_two = precondition(image_one)
    image_two = operate(search_two)
    gram = everywhere(
        jnp.stack(
            [
                inner(raw, raw),
                inner(image_one, raw),
                inner(image_one, image_one),
                inner(image_two, raw),
                inner(image_two, image_one),
                inner(image_two, image_two),
            ]
        )
    )
    weight_one, weight_two, ratio = weights(gram)
    return (weight_one * search_one + weight_two * search_two, ratio)


def solution(mesh):
    finer = Mesh(
        mesh.devices.reshape(4, 2, 2, 2, mesh.shape["gz"]), ("gx_0", "gx_1", "gy_0", "gy_1", "gz")
    )
    placed = (
        P(None, GX, Y, Z, None),
        P(None, GX, Y, Z),
        P(GX, Y, Z, None, None),
        P(GX, Y, Z, None, None),
        P(GX, Y, Z, None),
        P(GX, Y, Z, None),
        P(GX_GY_GZ, None),
    )
    return jax.shard_map(
        local,
        mesh=finer,
        in_specs=placed,
        out_specs=(P(None, GX, Y, Z, None), P()),
        check_vma=False,
    )
```

```python
import functools

import jax
import jax.numpy as jnp
from jax import lax
from jax.experimental import pallas as pl
from jax.experimental.pallas import tpu as pltpu
from jax.sharding import Mesh
from jax.sharding import PartitionSpec as P


X, C, Z = "gx_0", "gx_1", "gz"
GX, Y = (X, C), ("gy_0", "gy_1")
GX_GY_GZ = (*GX, *Y, Z)

EPSILON = 1e-06
SCALE = 2.0**-14
TILE = 256
SOME = 128


def shift(value, axis, step):
    count = lax.axis_size(axis)
    return lax.ppermute(value, axis, [(i, (i + step) % count) for i in range(count)])


def ends(blocks, dim):
    length, lanes = blocks.shape[dim], blocks.shape[-1]
    first = lax.slice_in_dim(blocks, 0, 1, axis=dim).reshape(-1, lanes)
    last = lax.slice_in_dim(blocks, length - 1, length, axis=dim).reshape(-1, lanes)
    return first, last


def swap_faces(blocks):
    first, last = ends(blocks, 1)
    lower = lax.axis_index(C) == 0
    inside = shift(jnp.where(lower, last, first), C, 1)
    peers = lax.axis_size(GX)
    up = [(i, i + 1) for i in range(1, peers - 1, 2)]
    across = lax.ppermute(
        jnp.where(lower, first, last), GX, up + [(b, a) for a, b in up]
    )
    return inside, across


def halo(blocks):
    inside, across = swap_faces(blocks)
    lower = lax.axis_index(C) == 0
    faces = [jnp.where(lower, across, inside), jnp.where(lower, inside, across)]
    for axis, dim in ((Y, 2), (Z, 3)):
        first, last = ends(blocks, dim)
        up = [(i, i + 1) for i in range(lax.axis_size(axis) - 1)]
        faces.append(lax.ppermute(last, axis, up))
        faces.append(lax.ppermute(first, axis, [(b, a) for a, b in up]))
    return faces


def inner(left, right):
    return jnp.sum(left * right, axis=(0, 1, 2, 3))


def weights(gram):
    raw_raw, one_raw, one_one, two_raw, two_one, two_two = (gram[i] for i in range(6))
    start_square = raw_raw / (SCALE * SCALE) + EPSILON
    start_norm = jnp.sqrt(start_square)
    size = start_norm * SCALE
    square = size * size
    kept = raw_raw / square
    along_one = one_raw / square
    rest_one = one_one / square - along_one * along_one * (2.0 - kept)
    rest_one = jnp.maximum(rest_one, 0.0) + EPSILON
    norm_two = jnp.sqrt(rest_one)
    kept_two = (rest_one - EPSILON) / rest_one
    shared = along_one * (1.0 - kept) / norm_two
    cross_two = (two_raw - along_one * one_raw) / (square * norm_two)
    along_two = (
        (two_one - along_one * two_raw) - along_one * (one_one - along_one * one_raw)
    ) / (square * rest_one)
    image_square = (two_two - along_one * (2.0 * two_one - along_one * one_one)) / (
        square * rest_one
    )
    rest_two = (
        image_square
        - cross_two * cross_two * (2.0 - kept)
        - along_two * along_two * (2.0 - kept_two)
        + 2.0 * cross_two * along_two * shared
    )
    norm_three = jnp.sqrt(jnp.maximum(rest_two, 0.0) + EPSILON)
    radius_one = jnp.sqrt(along_one * along_one + norm_two * norm_two)
    cosine_one = along_one / radius_one
    sine_one = norm_two / radius_one
    turned_one = cosine_one * cross_two + sine_one * along_two
    turned_two = cosine_one * along_two - sine_one * cross_two
    radius_two = jnp.sqrt(turned_two * turned_two + norm_three * norm_three)
    cosine_two = turned_two / radius_two
    sine_two = norm_three / radius_two
    coef_two = -cosine_two * sine_one * start_norm / radius_two
    coef_one = (cosine_one * start_norm - turned_one * coef_two) / radius_one
    weight_two = coef_two / (size * norm_two)
    weight_one = coef_one / size - along_one * weight_two
    return (weight_one, weight_two, sine_one * sine_two)


def local_kernel(place, order, own, *rest):
    faces, (factor, out, stacked, front, ring) = rest[:6], rest[6:]
    size = stacked.shape[0]
    own_count = own.shape[0]
    tiles = size // TILE
    half = size // 2

    def rows(i):
        return pl.ds(pl.multiple_of(i * TILE, TILE), TILE)

    stacked[:own_count] = own[...]
    inside, across, y_low, y_high, z_low, z_high = faces
    per_part = inside.shape[0] // 3
    lower = place[0] == 0
    for part in range(3):

        def layer(face):
            skip = face.shape[0] - inside.shape[0]
            return face[pl.ds(skip + part * per_part, per_part)]

        def put(k, value):
            ring[pl.ds((part * 6 + k) * per_part, per_part)] = value

        put(0, jnp.where(lower, layer(across), layer(inside)))
        put(1, jnp.where(lower, layer(inside), layer(across)))
        for k, face in enumerate((y_low, y_high, z_low, z_high)):
            value = layer(face)
            put(2 + k, jnp.where(place[1 + k] != 0, value, jnp.zeros_like(value)))

    def pick(k):
        some = pl.ds(pl.multiple_of(k * SOME, SOME), SOME)
        table = lax.broadcasted_iota(jnp.int32, (SOME, ring.shape[0]), 1) == order[some]
        stacked[pl.ds(pl.multiple_of(own_count + k * SOME, SOME), SOME)] = jnp.dot(
            table.astype(jnp.float32).astype(jnp.bfloat16),
            ring[...],
            preferred_element_type=jnp.float32,
        ).astype(jnp.bfloat16)

    pl.loop(0, order.shape[0] // SOME)(pick)

    def ahead(width, i):
        front[rows(i)] = jnp.dot(
            factor[rows(i), :width], stacked[:width], preferred_element_type=jnp.float32
        ).astype(jnp.bfloat16)

    def back(skip, j):
        piece = lax.dot_general(
            front[skip:], factor[skip:, rows(j)], contract_first, preferred_element_type=jnp.float32
        )
        out[rows(j)] = piece.T

    contract_first = (((0,), (0,)), ((), ()))
    middle = tiles // 2
    pl.loop(0, middle)(functools.partial(ahead, half))
    pl.loop(middle, tiles)(functools.partial(ahead, size))
    pl.loop(0, middle)(functools.partial(back, 0))
    pl.loop(middle, own_count // TILE)(functools.partial(back, half))


def local_solve(place, order, own, faces, factor):
    size, lanes = factor.shape[0], own.shape[-1]
    vmem = pl.BlockSpec(memory_space=pltpu.VMEM)
    return pl.pallas_call(
        local_kernel,
        out_shape=jax.ShapeDtypeStruct(own.shape, jnp.float32),
        in_specs=[pl.BlockSpec(memory_space=pltpu.SMEM)]
        + [vmem] * 9,
        out_specs=vmem,
        scratch_shapes=[
            pltpu.VMEM((size, lanes), jnp.bfloat16),
            pltpu.VMEM((size, lanes), jnp.bfloat16),
            pltpu.VMEM((6 * faces[0].shape[0], lanes), jnp.bfloat16),
        ],
        compiler_params=pltpu.CompilerParams(vmem_limit_bytes=24 * 1024 * 1024),
        name="local_solve",
    )(place, order, own, *faces, factor)


def stack_kernel(place, *refs):
    pieces, (mine, theirs) = refs[:-2], refs[-2:]
    rows, width = pieces[0].shape[0], mine.shape[1]
    for core, out in ((place[1], mine), (1 - place[1], theirs)):
        columns = pl.ds(pl.multiple_of(core * width, width), width)
        for step, piece in enumerate(pieces):
            out[pl.ds(step * rows, rows)] = piece[:, columns]


def stack(coarse_inverse, pieces):
    rows, width = pieces[0].shape
    count = len(pieces) + 1
    place = jnp.stack([lax.axis_index(X), lax.axis_index(C)]).astype(jnp.int32)
    whole = pl.BlockSpec((rows, width), lambda i, place: (0, 0))
    result = pl.BlockSpec((rows * count, width // 2), lambda i, place: (0, 0))
    shape = jax.ShapeDtypeStruct((rows * count, width // 2), coarse_inverse.dtype)
    return pl.pallas_call(
        stack_kernel,
        out_shape=(shape, shape),
        grid_spec=pltpu.PrefetchScalarGridSpec(
            num_scalar_prefetch=1,
            grid=(1,),
            in_specs=[pl.BlockSpec((rows, width), lambda i, place: (0, place[0]))]
            + [whole] * len(pieces),
            out_specs=(result, result),
        ),
        name="stack",
    )(place, coarse_inverse, *pieces)


def spread(coarse_inverse):
    rows, total = coarse_inverse.shape
    count = lax.axis_size(X)
    width = total // count
    at_x = lax.axis_index(X)
    pieces = []
    for step in range(1, count):
        place = (at_x + step) & (count - 1)
        piece = lax.dynamic_slice(coarse_inverse, (0, place * width), (rows, width))
        pieces.append(shift(piece, X, step))
    return stack(coarse_inverse, pieces)


def rolled(value, start, rows):
    doubled = jnp.concatenate([value, value])
    return lax.dynamic_slice(doubled, (start * rows, 0), value.shape)


def gathered(value, blocks):
    rows = value.shape[0]
    at_y, at_z = lax.axis_index(Y), lax.axis_index(Z)
    first, last = ends(blocks, 3)
    z_low = shift(jnp.concatenate([value, last]), Z, 1)
    z_high = shift(jnp.concatenate([value, first]), Z, -1)
    inside, across = swap_faces(blocks)
    pair = jnp.concatenate([z_low[:rows], value])
    three = jnp.concatenate([pair, z_high[:rows]])
    line = jnp.concatenate([shift(three, Z, 3), three, shift(pair, Z, -3)])
    line = rolled(line, (12 - at_z) & 7, rows)
    count = line.shape[0]
    first, last = ends(blocks, 2)
    opposite = shift(line, Y, 2)
    y_low = shift(jnp.concatenate([line, last]), Y, 1)
    y_high = shift(jnp.concatenate([line, first]), Y, 3)
    plane = jnp.concatenate([y_high[:count], opposite, y_low[:count], line])
    return rolled(plane, 3 - at_y, count), (inside, across, y_low, y_high, z_low, z_high)


def coarse_solve(stacks, whole, rows):
    theirs = shift(whole, C, 1)
    parts = jnp.dot(stacks[0], whole, preferred_element_type=jnp.float32)
    parts = parts + jnp.dot(stacks[1], theirs, preferred_element_type=jnp.float32)
    total = parts[:rows]
    for step in range(1, parts.shape[0] // rows):
        part = parts[step * rows : (step + 1) * rows]
        total = total + shift(part, X, -step)
    return total.astype(jnp.bfloat16)


def everywhere(partial):
    for axes in ((*GX, Y[1]), (Y[0], Z)):
        count = 1
        for axis in axes:
            count *= lax.axis_size(axis)
        copies = jnp.broadcast_to(partial[None], (count,) + partial.shape)
        partial = jnp.sum(lax.all_to_all(copies, axes, 0, 0, tiled=True), axis=0)
    return partial


def local(right_side, stiffness, local_factor, basis, coarse_map, margin_index, coarse_inverse):
    factor = local_factor.reshape(local_factor.shape[-2:])
    basis_count = basis.shape[-2]
    coarse_ids = coarse_map.reshape(-1)
    order = margin_index.reshape(-1, 1)
    placement = (
        coarse_ids[None, :] == lax.broadcasted_iota(jnp.int32, (basis_count, basis_count), 0)
    ).astype(jnp.bfloat16)
    functions = jnp.dot(
        placement, basis.reshape(basis.shape[-2:]), preferred_element_type=jnp.float32
    ).astype(jnp.bfloat16)
    contract_first = (((0,), (0,)), ((), ()))
    at_y, at_z = lax.axis_index(Y), lax.axis_index(Z)
    place = jnp.stack(
        [
            lax.axis_index(C),
            at_y > 0,
            at_y < lax.axis_size(Y) - 1,
            at_z > 0,
            at_z < lax.axis_size(Z) - 1,
        ]
    ).astype(jnp.int32)
    diagonal = 6.0 + stiffness[..., None]
    stacks = spread(coarse_inverse)

    def precondition(field):
        rounded = field.astype(jnp.bfloat16)
        own_rows = rounded.reshape(-1, rounded.shape[-1])
        placed = jnp.dot(functions, own_rows, preferred_element_type=jnp.float32).astype(
            jnp.bfloat16
        )
        whole, faces = gathered(placed, rounded)
        local_part = local_solve(place, order, own_rows, faces, factor)
        solved = coarse_solve(stacks, whole, basis_count)
        coarse_part = lax.dot_general(
            functions, solved, contract_first, preferred_element_type=jnp.float32
        )
        return (local_part + coarse_part).reshape(field.shape)

    def operate(field):
        faces = halo(field.astype(jnp.bfloat16))
        beside = None
        for dim in (1, 2, 3):
            shape = list(field.shape)
            shape[dim] = 1
            low, high = (
                face.astype(field.dtype).reshape(shape) for face in faces[2 * dim - 2 : 2 * dim]
            )
            length = field.shape[dim]
            before = jnp.concatenate([low, lax.slice_in_dim(field, 0, length - 1, axis=dim)], dim)
            after = jnp.concatenate([lax.slice_in_dim(field, 1, length, axis=dim), high], dim)
            beside = before + after if beside is None else beside + before + after
        return diagonal * field - beside

    raw = right_side * SCALE
    search_one = precondition(raw)
    image_one = operate(search_one)
    search_two = precondition(image_one)
    image_two = operate(search_two)
    gram = everywhere(
        jnp.stack(
            [
                inner(raw, raw),
                inner(image_one, raw),
                inner(image_one, image_one),
                inner(image_two, raw),
                inner(image_two, image_one),
                inner(image_two, image_two),
            ]
        )
    )
    weight_one, weight_two, ratio = weights(gram)
    return (weight_one * search_one + weight_two * search_two, ratio)


def solution(mesh):
    finer = Mesh(
        mesh.devices.reshape(4, 2, 2, 2, mesh.shape["gz"]), ("gx_0", "gx_1", "gy_0", "gy_1", "gz")
    )
    placed = (
        P(None, GX, Y, Z, None),
        P(None, GX, Y, Z),
        P(GX, Y, Z, None, None),
        P(GX, Y, Z, None, None),
        P(GX, Y, Z, None),
        P(GX, Y, Z, None),
        P(GX_GY_GZ, None),
    )
    return jax.shard_map(
        local,
        mesh=finer,
        in_specs=placed,
        out_specs=(P(None, GX, Y, Z, None), P()),
        check_vma=False,
    )
```
